256 devices in a mesh: req: 32 (over x, z), tp: 8 (over y, core).
Axes of the slice: x: 4, y: 4, z: 8, core: 2. Of those that a mesh axis runs over, the one named last changes fastest.
Arguments:
- embeds: bfloat16 [4, 256, 2048], P(None, 'req'), may hold values from -6 to 6
- attn_gain: float32 [2048], replicated, may hold values from 0.1 to 1.9
- qkv_weight: bfloat16 [2048, 3, 2048], P(None, None, 'tp'), may hold values from -0.125 to 0.125
- query_gain: float32 [2048], P('tp'), may hold values from 0.1 to 1.9
- key_gain: float32 [2048], P('tp'), may hold values from 1.5 to 3
- out_weight: bfloat16 [2048, 2048], P('tp'), may hold values from -0.125 to 0.125
- mlp_gain: float32 [2048], replicated, may hold values from 0.1 to 1.9
- router_weight: bfloat16 [2048, 64], replicated, may hold values from -0.25 to 0.25
- gate_up: bfloat16 [64, 2048, 2, 1024], P('req', None, None, 'tp'), may hold values from -0.125 to 0.125
- down_weight: bfloat16 [64, 1024, 2048], P('req', 'tp'), may hold values from -0.1875 to 0.1875
- cache_keys: bfloat16 [131072, 2048], P('req', 'tp')
- cache_values: bfloat16 [131072, 2048], P('req', 'tp'), may hold values from -6 to 6
- tail_keys: bfloat16 [256, 4, 2048], P('req', None, 'tp'), may hold values from -16 to 16
- tail_values: bfloat16 [256, 4, 2048], P('req', None, 'tp'), may hold values from -6 to 6
- parents: int32 [4, 256], P(None, 'req'), may hold values from 0 to 7
- routes: int32 [4, 256, 8], P(None, 'req'), may hold values from 0 to 63, all different within a row; in each aligned block of 8 rows (0 to 7, 8 to 15, ..., all dimensions but the last counted through in order) at most 5 rows name the same one
- group_lengths: int32 [32], replicated, may hold values from 1 to 16384, as said below
- slot_group: int32 [1024], P('req'), may hold values from -1 to 31, as said below
- slot_index: int32 [1024], P('req'), may hold values from 0 to 127, as said below
Outputs:
- hidden_out: bfloat16 [4, 256, 2048], P(None, 'req', 'tp')
- keys_out: bfloat16 [256, 8, 2048], P('req', None, 'tp')
- values_out: bfloat16 [256, 8, 2048], P('req', None, 'tp')
The draws below stay inside these ranges and needn't reach their ends.
Inputs may be any that keep to these rules, and one draw needn't show every extreme that they name: `parents`: a beam's parent is numbered within its own group. `routes`: each row names 8 different experts; at each step the rows of one index of req (aligned blocks of 8 rows) name one expert at most 5 times, a bound that some block reaches. `group_lengths`: a group of length n holds (n + 127) // 128 pieces. `slot_group`: -1 marks an empty slot; every piece of every group stands in exactly one slot. `slot_index`: 0 in empty slots.
All inputs are finite; a program needn't handle non-finite values.
Results may differ from the reference program's by a relative error of at most 0.015.
The reference program's roundings to bfloat16 on the way count: a program that leaves them out, or rounds other values in their place, can miss the bound.
Values may be sent and summed in bfloat16 or wider, within the bound.
A program may use at most 128 MiB of HBM per device.

```python
import math
import jax
import jax.numpy as jnp
import numpy as np
from jax import lax

D = 2048
HEADS = 16
HD = 128
EXPERTS = 64
FF = 1024
TOP = 8
BEAMS = 8
GROUPS_DEV = 1
SLOTS_DEV = 32
PIECE = 128
CAP = 5
STEPS = 4
HIST = 4
GROUPS = 32
ROWS = 256
SLOTS = 1024
MAXP = 128
OTHERP = 28
TAIL = 8
N_REQ = 32


def shared_layout(key):
    base_key = jax.random.fold_in(key, 101)
    count_key = jax.random.fold_in(base_key, 1)
    longest_key = jax.random.fold_in(base_key, 2)
    fill_key = jax.random.fold_in(base_key, 3)
    order_key = jax.random.fold_in(base_key, 4)
    group_ids = jnp.arange(GROUPS, dtype=jnp.int32)
    counts = jax.random.randint(count_key, (GROUPS,), 1, OTHERP + 1, dtype=jnp.int32)
    longest = jax.random.randint(longest_key, (), 0, GROUPS, dtype=jnp.int32)
    counts = jnp.where(group_ids == longest, MAXP, counts)
    fills = jax.random.randint(fill_key, (GROUPS,), 1, PIECE + 1, dtype=jnp.int32)
    fills = jnp.where(group_ids == longest, PIECE, fills)
    order = jax.random.permutation(order_key, SLOTS)
    return (counts, fills, order)


def slot_table(key):
    counts, fills, order = shared_layout(key)
    piece_of_slot = jnp.argsort(order).astype(jnp.int32)
    ends = jnp.cumsum(counts).astype(jnp.int32)
    starts = ends - counts
    filled = piece_of_slot < ends[-1]
    owner = jnp.sum((piece_of_slot[:, None] >= ends[None, :]).astype(jnp.int32), axis=1)
    owner_safe = jnp.minimum(owner, GROUPS - 1)
    groups_out = jnp.where(filled, owner_safe, -1).astype(jnp.int32)
    index_out = jnp.where(filled, piece_of_slot - starts[owner_safe], 0).astype(jnp.int32)
    return (groups_out, index_out)


def draw_group_lengths(key, part):
    counts, fills, order = shared_layout(key)
    return ((counts - 1) * PIECE + fills).astype(jnp.int32)


def draw_slot_group(key, part):
    return slot_table(key)[0]


def draw_slot_index(key, part):
    return slot_table(key)[1]


def draw_cache_keys(key, part):
    first_key = jax.random.fold_in(key, 201)
    shape = (SLOTS * PIECE, D)
    return jnp.clip(2.5 * jax.random.normal(first_key, shape, jnp.float32), -16.0, 16.0).astype(jnp.bfloat16)


def plant(values, key, least, top_value):
    longest = values.shape.index(max(values.shape))
    spots = []
    for shift in (0, 1):
        where = [jax.random.randint(jax.random.fold_in(key, axis), (), 0, length) for axis, length in enumerate(values.shape)]
        where[longest] = (where[longest] + shift) % values.shape[longest]
        spots.append(tuple(where))
    return values.at[spots[0]].set(least).at[spots[1]].set(top_value)


def steps_of(rng, extent, cuts, smallest, top_value):
    gain, own = 1.0, jax.random.fold_in(rng, 6)
    for axis_at, shards_of in cuts:
        steps = jnp.exp(jax.random.uniform(jax.random.fold_in(own, axis_at), (shards_of,), jnp.float32, smallest / len(cuts), top_value / len(cuts)))
        gain = gain * jnp.repeat(steps, extent[axis_at] // shards_of).reshape([-1 if axis == axis_at else 1 for axis in range(len(extent))])
    return gain


def deal_out(key, own, number, rows, number_of, top, reach, skew):
    order = jax.random.permutation(key, number_of)
    crowded, ordinary = load_shares(number_of, rows * top, reach, skew, True), load_shares(number_of, rows * top, reach, skew, False)
    places = jnp.arange(number_of)

    def named(tallies, rotation):
        used = int((tallies > 0).sum())
        fixed = max(1, used // 4)
        moved = fixed + (places - fixed + rotation * (used - fixed)) % max(1, number_of - fixed)
        return jnp.zeros((number_of,), jnp.int32).at[order[jnp.where(places < fixed, places, moved)]].set(jnp.asarray(tallies, jnp.int32))

    tallies = jnp.where(number % 4 == 0, named(crowded, number // 4), named(ordinary, number - number // 4 - 1))
    mixed = jax.random.permutation(jax.random.fold_in(own, 3), number_of)
    giver, receiver = mixed[0:number_of // 2 * 2:2], mixed[1:number_of // 2 * 2:2]
    room = jnp.minimum(tallies[giver] - 1, reach - tallies[receiver]) // 2
    room = jnp.where((giver == order[0]) | (receiver == order[0]) | (tallies[receiver] == 0), 0, jnp.maximum(room, 0))
    moved = jax.random.randint(jax.random.fold_in(own, 4), (number_of // 2,), 0, 1 << 20) % (room + 1)
    tallies = tallies.at[giver].add(-moved).at[receiver].add(moved)
    items = jnp.searchsorted(jnp.cumsum(tallies), jnp.arange(rows * top), side="right").astype(jnp.int32)
    listing = items.reshape(top, rows).T
    listing = listing[jax.random.permutation(jax.random.fold_in(own, 1), rows)]
    rotation = jax.random.randint(jax.random.fold_in(own, 2), (rows, 1), 0, top)
    return jnp.take_along_axis(listing, (jnp.arange(top)[None, :] + rotation) % top, axis=1)


def load_shares(number_of, total, bound, lean, full):
    loads = [(1 << 20) // math.isqrt(rank ** lean) + 1 for rank in range(1, number_of + 1)]
    largest = bound if full else min(bound, max(-(-total // number_of), total * loads[0] // sum(loads)))
    least = 1 if total - largest >= number_of - 1 else 0
    holding, spare = [largest] + [least] * (number_of - 1), total - largest - least * (number_of - 1)
    while spare > 0:
        free = [i for i in range(1, number_of) if holding[i] < largest] or [i for i in range(1, number_of) if holding[i] < bound]
        whole, left = sum([loads[i] for i in free]), spare
        for i in free:
            more = min(bound - holding[i], max(1, left * loads[i] // whole), spare)
            holding[i] = holding[i] + more
            spare = spare - more
    return np.array(holding)


def scatter_about(own_key, dims, spread, bound, pieces=(), held_as=jnp.bfloat16):
    level = steps_of(own_key, dims, pieces, -0.22, 0.18) if pieces else 1.0
    drawn = jax.random.normal(own_key, dims, jnp.float32) * spread * level
    return jnp.minimum(jnp.maximum(drawn, -bound), bound).astype(held_as)


def setup_inputs(seed: int = 0) -> dict:
    splits = jax.random.split(jax.random.key(seed), 20)
    embeds = scatter_about(splits[0], (STEPS, ROWS, D), 1.0, 6.0, ((1, 32),))
    attn_gain = jnp.clip(1.0 + 0.18 * jax.random.normal(splits[1], (D,), jnp.float32), 0.1, 1.9)
    qkv_weight = scatter_about(splits[2], (D, 3, D), D ** -0.5, 0.125, ((2, 8),))
    query_gain = jnp.clip(1.0 + 0.18 * jax.random.normal(splits[3], (D,), jnp.float32), 0.1, 1.9)
    key_gain = jnp.clip(jnp.exp(math.log(3.0) - 0.6931472 * jax.random.uniform(splits[4], (D,), jnp.float32) ** steps_of(splits[4], (D,), ((0, 8),), -0.2, 0.2)), 1.5, 3.0)
    out_weight = scatter_about(splits[5], (D, D), D ** -0.5, 0.125, ((0, 8),))
    mlp_gain = jnp.clip(1.0 + 0.18 * jax.random.normal(splits[6], (D,), jnp.float32), 0.1, 1.9)
    router_weight = scatter_about(splits[7], (D, EXPERTS), (D // 4) ** -0.5, 0.25)
    gate_up = scatter_about(splits[8], (EXPERTS, D, 2, FF), D ** -0.5, 0.125, ((0, 32), (3, 8)))
    down_weight = scatter_about(splits[9], (EXPERTS, FF, D), FF ** -0.5, 0.1875, ((0, 32), (1, 8)))
    cache_keys = draw_cache_keys(jax.random.fold_in(splits[19], 71), 0)
    cache_values = scatter_about(splits[11], (SLOTS * PIECE, D), 1.0, 6.0, ((0, 32), (1, 8)))
    tail_keys = scatter_about(splits[12], (ROWS, HIST, D), 2.5, 16.0, ((0, 32), (2, 8)))
    tail_values = scatter_about(splits[13], (ROWS, HIST, D), 1.0, 6.0, ((0, 32), (2, 8)))
    parents = plant(jax.random.randint(splits[14], (STEPS, ROWS), 0, BEAMS), jax.random.fold_in(splits[14], 1), 0, BEAMS - 1).astype(jnp.int32)
    routes_keys = jax.random.split(jax.random.fold_in(splits[15], 1), STEPS * ROWS // (GROUPS_DEV * BEAMS))
    routes_turns = jax.random.permutation(jax.random.fold_in(splits[15], 3), STEPS * ROWS // (GROUPS_DEV * BEAMS))
    routes = jax.vmap(lambda own, number: deal_out(jax.random.fold_in(splits[15], 2), own, number, GROUPS_DEV * BEAMS, EXPERTS, TOP, CAP, 2))(routes_keys, routes_turns).reshape((STEPS, ROWS, TOP))
    group_lengths = draw_group_lengths(jax.random.fold_in(splits[19], 71), 0)
    slot_group = draw_slot_group(jax.random.fold_in(splits[19], 71), 0)
    slot_index = draw_slot_index(jax.random.fold_in(splits[19], 71), 0)
    return dict(embeds=embeds, attn_gain=attn_gain, qkv_weight=qkv_weight, query_gain=query_gain, key_gain=key_gain, out_weight=out_weight, mlp_gain=mlp_gain, router_weight=router_weight, gate_up=gate_up, down_weight=down_weight, cache_keys=cache_keys, cache_values=cache_values, tail_keys=tail_keys, tail_values=tail_values, parents=parents, routes=routes, group_lengths=group_lengths, slot_group=slot_group, slot_index=slot_index)


eps = 1e-05
floor_value = -1e+30

def norm_rows(values, scale_gain):
    mean_square = lax.optimization_barrier(jnp.mean(values * values, axis=-1, keepdims=True))
    return values * lax.rsqrt(mean_square + eps) * scale_gain

def rotate_heads(values, positions):
    half_size = values.shape[-1] // 2
    freqs = jnp.exp(jnp.arange(half_size, dtype=jnp.float32) * (-2.0 * math.log(10000.0) / values.shape[-1]))
    angles = positions.astype(jnp.float32)[:, None] * freqs[None, :]
    cosine = jnp.cos(angles)[:, None, :]
    sine = jnp.sin(angles)[:, None, :]
    first_half = values[..., :half_size]
    second_half = values[..., half_size:]
    return jnp.concatenate([first_half * cosine - second_half * sine, second_half * cosine + first_half * sine], axis=-1)

def piece_partials(query_groups, lengths, keys_block, values_block, groups_block, index_block):
    safe_group = jnp.maximum(groups_block, 0)
    queries_here = query_groups[safe_group]
    scores = jnp.einsum('sbhd,sphd->sbhp', queries_here.astype(jnp.float32), keys_block.astype(jnp.float32)) * (1.0 / math.sqrt(HD))
    places = index_block[:, None] * PIECE + jnp.arange(PIECE, dtype=jnp.int32)[None, :]
    live = (groups_block[:, None] >= 0) & (places < lengths[safe_group][:, None])
    live_mask = live[:, None, None, :]
    scores = jnp.where(live_mask, scores, floor_value)
    peak = lax.optimization_barrier(jnp.max(scores, axis=-1))
    weights = jnp.where(live_mask, jnp.exp(scores - peak[..., None]), 0.0)
    weight_sum = lax.optimization_barrier(jnp.sum(weights, axis=-1))
    blended = jnp.einsum('sbhp,sphd->sbhd', weights.astype(jnp.bfloat16).astype(jnp.float32), values_block.astype(jnp.float32))
    return (peak, weight_sum, blended)

def reference(embeds, attn_gain, qkv_weight, query_gain, key_gain, out_weight, mlp_gain, router_weight, gate_up, down_weight, cache_keys, cache_values, tail_keys, tail_values, parents, routes, group_lengths, slot_group, slot_index):
    row_count = GROUPS * BEAMS
    block_rows = GROUPS_DEV * BEAMS
    row_group = jnp.arange(row_count, dtype=jnp.int32) // BEAMS
    keys_all = jnp.concatenate([tail_keys, jnp.zeros((row_count, STEPS, D), jnp.bfloat16)], axis=1)
    values_all = jnp.concatenate([tail_values, jnp.zeros((row_count, STEPS, D), jnp.bfloat16)], axis=1)
    keys_blocks = cache_keys.reshape(N_REQ, SLOTS_DEV, PIECE, HEADS, HD)
    values_blocks = cache_values.reshape(N_REQ, SLOTS_DEV, PIECE, HEADS, HD)
    groups_blocks = slot_group.reshape(N_REQ, SLOTS_DEV)
    index_blocks = slot_index.reshape(N_REQ, SLOTS_DEV)
    group_hot = slot_group[None, :] == jnp.arange(GROUPS, dtype=jnp.int32)[:, None]
    hot_float = group_hot.astype(jnp.float32)
    expert_ids = jnp.arange(EXPERTS, dtype=jnp.int32)
    block_ids = jnp.broadcast_to(jnp.arange(N_REQ, dtype=jnp.int32)[:, None], (N_REQ, block_rows * TOP))
    results_list = []
    for step_index in range(STEPS):
        inputs = embeds[step_index].astype(jnp.float32)
        normed = norm_rows(inputs, attn_gain).astype(jnp.bfloat16)
        proj = jnp.dot(normed, qkv_weight.reshape(D, 3 * D), preferred_element_type=jnp.float32).reshape(row_count, 3, D)
        positions = group_lengths[row_group] + HIST + step_index
        query = rotate_heads(norm_rows(proj[:, 0], query_gain).reshape(row_count, HEADS, HD), positions).astype(jnp.bfloat16)
        key_new = rotate_heads(norm_rows(proj[:, 1], key_gain).reshape(row_count, HEADS, HD), positions).astype(jnp.bfloat16)
        value_new = proj[:, 2].astype(jnp.bfloat16)
        source_rows = row_group * BEAMS + parents[step_index]
        keys_all = keys_all[source_rows].at[:, HIST + step_index].set(key_new.reshape(row_count, D))
        values_all = values_all[source_rows].at[:, HIST + step_index].set(value_new)
        query_groups = query.reshape(GROUPS, BEAMS, HEADS, HD)

        def one_block(block_items):
            return piece_partials(query_groups, group_lengths, block_items[0], block_items[1], block_items[2], block_items[3])
        peak, weight_sum, blended = lax.map(one_block, (keys_blocks, values_blocks, groups_blocks, index_blocks))
        peak = peak.reshape(SLOTS, BEAMS, HEADS)
        weight_sum = weight_sum.reshape(SLOTS, BEAMS, HEADS)
        blended = blended.reshape(SLOTS, BEAMS, HEADS, HD)
        group_peak = lax.optimization_barrier(jnp.max(jnp.where(group_hot[:, :, None, None], peak[None], floor_value), axis=1))
        own_peak = group_peak[jnp.maximum(slot_group, 0)]
        factor = jnp.where((slot_group >= 0)[:, None, None], jnp.exp(peak - own_peak), 0.0)
        cache_sum = jnp.einsum('gs,sbh->gbh', hot_float, factor * weight_sum, precision=lax.Precision.HIGHEST)
        cache_blend = jnp.einsum('gs,sbhd->gbhd', hot_float, factor[..., None] * blended, precision=lax.Precision.HIGHEST)
        tail_k = keys_all.reshape(row_count, TAIL, HEADS, HD)
        tail_v = values_all.reshape(row_count, TAIL, HEADS, HD)
        tail_scores = jnp.einsum('rhd,rjhd->rhj', query.astype(jnp.float32), tail_k.astype(jnp.float32)) * (1.0 / math.sqrt(HD))
        tail_live = (jnp.arange(TAIL, dtype=jnp.int32) <= HIST + step_index)[None, None, :]
        tail_scores = jnp.where(tail_live, tail_scores, floor_value)
        tail_peak = lax.optimization_barrier(jnp.max(tail_scores, axis=-1))
        tail_weights = jnp.where(tail_live, jnp.exp(tail_scores - tail_peak[..., None]), 0.0)
        tail_sum = lax.optimization_barrier(jnp.sum(tail_weights, axis=-1))
        tail_blend = jnp.einsum('rhj,rjhd->rhd', tail_weights.astype(jnp.bfloat16).astype(jnp.float32), tail_v.astype(jnp.float32))
        cache_peak = group_peak.reshape(row_count, HEADS)
        best_peak = jnp.maximum(cache_peak, tail_peak)
        cache_factor = jnp.exp(cache_peak - best_peak)
        tail_factor = jnp.exp(tail_peak - best_peak)
        numer = cache_factor[..., None] * cache_blend.reshape(row_count, HEADS, HD) + tail_factor[..., None] * tail_blend
        denom = cache_factor * cache_sum.reshape(row_count, HEADS) + tail_factor * tail_sum
        context = (numer / denom[..., None]).reshape(row_count, D).astype(jnp.bfloat16)
        hidden = inputs + jnp.dot(context, out_weight, preferred_element_type=jnp.float32)
        mlp_in = norm_rows(hidden, mlp_gain).astype(jnp.bfloat16)
        logits = jnp.dot(mlp_in, router_weight, preferred_element_type=jnp.float32)
        chosen = jnp.take_along_axis(logits, routes[step_index], axis=1)
        probs = jax.nn.softmax(chosen, axis=-1)
        picks = routes[step_index].reshape(N_REQ, block_rows * TOP)
        expert_hot = (picks[..., None] == expert_ids[None, None, :]).astype(jnp.int32)
        ranks = lax.optimization_barrier(jnp.sum((jnp.cumsum(expert_hot, axis=1) - expert_hot) * expert_hot, axis=-1)).astype(jnp.int32)
        sent_rows = jnp.repeat(mlp_in, TOP, axis=0).reshape(N_REQ, block_rows * TOP, D)
        buffer = jnp.zeros((EXPERTS, N_REQ, CAP, D), jnp.bfloat16).at[picks, block_ids, ranks].set(sent_rows)

        def one_expert(expert_items):
            rows_in, weights_in, weights_out = expert_items
            gate_and_up = jnp.dot(rows_in.reshape(N_REQ * CAP, D), weights_in.reshape(D, 2 * FF), preferred_element_type=jnp.float32).reshape(N_REQ * CAP, 2, FF)
            activated = (jax.nn.silu(gate_and_up[:, 0]) * gate_and_up[:, 1]).astype(jnp.bfloat16)
            return jnp.dot(activated, weights_out, preferred_element_type=jnp.float32).astype(jnp.bfloat16).reshape(N_REQ, CAP, D)
        expert_results = lax.map(one_expert, (buffer, gate_up, down_weight))
        picked = expert_results[picks, block_ids, ranks].reshape(row_count, TOP, D)
        mixture = lax.optimization_barrier(jnp.sum(probs[..., None] * picked.astype(jnp.float32), axis=1))
        results_list.append((hidden + mixture).astype(jnp.bfloat16))
    return (jnp.stack(results_list), keys_all, values_all)
```

```python
import math

import jax
import jax.numpy as jnp
from jax import lax
from jax.experimental import pallas as pl
from jax.experimental.pallas import tpu as pltpu
from jax.sharding import PartitionSpec as P

HD = 128
BEAMS = 8
PIECE = 128
STEPS = 4
HIST = 4
TAIL = 8
SLOT_BLOCK = 4

eps = 1e-05
floor_value = -1e30
scale = 1.0 / math.sqrt(HD)


def norm_rows(values, scale_gain):
    mean_square = jnp.mean(values * values, axis=-1, keepdims=True)
    return values * lax.rsqrt(mean_square + eps) * scale_gain


def rotate_heads(values, positions):
    half_size = values.shape[-1] // 2
    freqs = jnp.exp(
        jnp.arange(half_size, dtype=jnp.float32) * (-2.0 * math.log(10000.0) / values.shape[-1])
    )
    angles = positions.astype(jnp.float32)[:, None] * freqs[None, :]
    cosine = jnp.cos(angles)[:, None, :]
    sine = jnp.sin(angles)[:, None, :]
    first_half = values[..., :half_size]
    second_half = values[..., half_size:]
    return jnp.concatenate(
        [first_half * cosine - second_half * sine, second_half * cosine + first_half * sine],
        axis=-1,
    )


def dot_t(left, right):
    return lax.dot_general(
        left, right, (((1,), (1,)), ((), ())), preferred_element_type=jnp.float32
    )


def cache_kernel(groups_ref, index_ref, lengths_ref, q_ref, k_ref, v_ref, out_ref, acc):
    rows, cols = q_ref.shape[1], q_ref.shape[2]
    heads = cols // HD
    step = pl.program_id(0)
    lane = lax.broadcasted_iota(jnp.int32, (rows, PIECE), 1)

    @pl.when(step == 0)
    def _():
        @pl.loop(0, q_ref.shape[0])
        def _(g):
            acc[g, :, :cols] = jnp.zeros((rows, cols), jnp.float32)
            acc[g, :, cols:] = jnp.where(lane < heads, floor_value, 0.0)

    found = []
    for j in range(SLOT_BLOCK):
        slot = step * SLOT_BLOCK + j
        group = groups_ref[slot]
        safe = jnp.maximum(group, 0)
        limit = jnp.where(group >= 0, lengths_ref[safe] - index_ref[slot] * PIECE, 0)
        live = lane < limit
        here = pl.ds(j * PIECE, PIECE)
        parts = []
        for h in range(heads):
            cut = pl.ds(h * HD, HD)
            scores = dot_t(q_ref[safe, :, cut], k_ref[here, cut]) * scale
            scores = jnp.where(live, scores, floor_value)
            peak = jnp.max(scores, axis=1, keepdims=True)
            weights = jnp.where(live, jnp.exp(scores - peak), 0.0)
            total = jnp.sum(weights, axis=1, keepdims=True)
            blend = jnp.dot(
                weights.astype(jnp.bfloat16), v_ref[here, cut], preferred_element_type=jnp.float32
            )
            parts.append((peak, total, blend))
        found.append((safe, parts))
    for safe, parts in found:
        stat = acc[safe, :, cols:]
        fresh = stat
        for h, (peak, total, blend) in enumerate(parts):
            cut = pl.ds(h * HD, HD)
            old = stat[:, h : h + 1]
            best = jnp.maximum(old, peak)
            old_factor = jnp.exp(old - best)
            new_factor = jnp.exp(peak - best)
            acc[safe, :, cut] = old_factor * acc[safe, :, cut] + new_factor * blend
            sums = old_factor * stat[:, heads + h : heads + h + 1] + new_factor * total
            fresh = jnp.where(lane == h, best, jnp.where(lane == heads + h, sums, fresh))
        acc[safe, :, cols:] = fresh

    @pl.when(step == pl.num_programs(0) - 1)
    def _():
        words = 2 * heads

        @pl.loop(0, q_ref.shape[0])
        def _(g):
            out_ref[g, :, :cols] = acc[g, :, :cols].astype(jnp.bfloat16)
            stat = acc[g, :, cols:]
            first = stat.astype(jnp.bfloat16).astype(jnp.float32)
            second = (stat - first).astype(jnp.bfloat16).astype(jnp.float32)
            third = stat - first - second
            packed = jnp.where(
                lane < words,
                first,
                jnp.where(
                    lane < 2 * words,
                    pltpu.roll(second, words, 1),
                    jnp.where(lane < 3 * words, pltpu.roll(third, 2 * words, 1), 0.0),
                ),
            )
            out_ref[g, :, cols:] = packed.astype(jnp.bfloat16)


def cache_partials(query_groups, cache_keys, cache_values, slot_group, slot_index, lengths):
    groups, rows, cols = query_groups.shape
    slots = slot_group.shape[0]
    block = SLOT_BLOCK * PIECE
    return pl.pallas_call(
        cache_kernel,
        out_shape=jax.ShapeDtypeStruct((groups, rows, cols + 128), jnp.bfloat16),
        grid_spec=pltpu.PrefetchScalarGridSpec(
            num_scalar_prefetch=3,
            grid=(slots // SLOT_BLOCK,),
            in_specs=[
                pl.BlockSpec((groups, rows, cols), lambda i, *_: (0, 0, 0)),
                pl.BlockSpec((block, cols), lambda i, *_: (i, 0)),
                pl.BlockSpec((block, cols), lambda i, *_: (i, 0)),
            ],
            out_specs=pl.BlockSpec((groups, rows, cols + 128), lambda i, *_: (0, 0, 0)),
            scratch_shapes=[pltpu.VMEM((groups, rows, cols + 128), jnp.float32)],
        ),
    )(slot_group, slot_index, lengths, query_groups, cache_keys, cache_values)


def merge_kernel(part_ref, q_ref, k_ref, v_ref, live_ref, out_ref):
    sources, rows = part_ref.shape[0], part_ref.shape[1]
    cols = q_ref.shape[1]
    heads = cols // HD
    words = 2 * heads
    live = live_ref[...] > 0.5
    stats = []
    for s in range(sources):
        packed = part_ref[s, :, cols:].astype(jnp.float32)
        stats.append(
            packed + pltpu.roll(packed, 128 - words, 1) + pltpu.roll(packed, 128 - 2 * words, 1)
        )
    top = stats[0]
    for s in range(1, sources):
        top = jnp.maximum(top, stats[s])
    for h in range(heads):
        cut = pl.ds(h * HD, HD)
        scores = jnp.where(live, dot_t(q_ref[:, cut], k_ref[:, cut]) * scale, floor_value)
        peak = jnp.max(scores, axis=1, keepdims=True)
        weights = jnp.where(live, jnp.exp(scores - peak), 0.0)
        total = jnp.sum(weights, axis=1, keepdims=True)
        blend = jnp.dot(
            weights.astype(jnp.bfloat16), v_ref[:, cut], preferred_element_type=jnp.float32
        )
        best = jnp.maximum(peak, top[:, h : h + 1])
        factor = jnp.exp(peak - best)
        numer = factor * blend
        denom = factor * total
        for s in range(sources):
            factor = jnp.exp(stats[s][:, h : h + 1] - best)
            numer = numer + factor * part_ref[s, :, cut].astype(jnp.float32)
            denom = denom + factor * stats[s][:, heads + h : heads + h + 1]
        out_ref[:, cut] = (numer / denom).astype(jnp.bfloat16)


def merge_partials(parts, query, keys_all, values_all, live):
    return pl.pallas_call(
        merge_kernel,
        out_shape=jax.ShapeDtypeStruct(query.shape, jnp.bfloat16),
        in_specs=[pl.BlockSpec(memory_space=pltpu.VMEM)] * 5,
        out_specs=pl.BlockSpec(memory_space=pltpu.VMEM),
    )(parts, query, keys_all, values_all, live)


def ancestry(parents):
    beams = jnp.arange(BEAMS, dtype=jnp.int32)

    def follow(table, where):
        return jnp.sum(jnp.where(where[:, None] == beams[None, :], table[None, :], 0), axis=1)

    back = []
    for t in range(STEPS):
        rows = [beams, parents[t]]
        for k in range(2, t + 2):
            rows.append(follow(back[t - 1][k - 1], parents[t]))
        back.append(rows)
    sources = []
    for t in range(STEPS):
        first = back[t][t + 1] * HIST
        columns = [first + j for j in range(HIST)]
        for u in range(STEPS):
            if u <= t:
                columns.append(BEAMS * HIST + u * BEAMS + back[t][t - u])
            else:
                columns.append(jnp.full((BEAMS,), -1, jnp.int32))
        sources.append(jnp.stack(columns, axis=1))
    return jnp.stack(sources)


def body(
    embeds,
    attn_gain,
    qkv_weight,
    query_gain,
    key_gain,
    out_weight,
    mlp_gain,
    router_weight,
    gate_up,
    down_weight,
    cache_keys,
    cache_values,
    tail_keys,
    tail_values,
    parents,
    routes,
    group_lengths,
    slot_group,
    slot_index,
):
    req_place = lax.axis_index("req")
    tp_place = lax.axis_index("tp")
    local_rows = embeds.shape[1]
    width = embeds.shape[2]
    col_width = qkv_weight.shape[2]
    heads_here = col_width // HD
    experts_here = gate_up.shape[0]
    experts_all = router_weight.shape[1]
    hidden_here = gate_up.shape[3]
    rows = STEPS * local_rows

    routes_all = lax.all_gather(
        routes.reshape(rows, routes.shape[2]), "req", axis=0, tiled=True
    )

    inputs = embeds.reshape(rows, width).astype(jnp.float32)
    normed = norm_rows(inputs, attn_gain).astype(jnp.bfloat16)
    proj = jnp.dot(
        normed, qkv_weight.reshape(width, 3 * col_width), preferred_element_type=jnp.float32
    )
    query_raw = proj[:, :col_width]
    key_raw = proj[:, col_width : 2 * col_width]
    value_new = proj[:, 2 * col_width :].astype(jnp.bfloat16)
    squares = lax.psum(
        jnp.stack([jnp.sum(query_raw * query_raw, axis=1), jnp.sum(key_raw * key_raw, axis=1)]),
        "tp",
    )
    query_normed = query_raw * lax.rsqrt(squares[0][:, None] / width + eps) * query_gain
    key_normed = key_raw * lax.rsqrt(squares[1][:, None] / width + eps) * key_gain
    own_length = lax.dynamic_index_in_dim(group_lengths, req_place, 0, False)
    positions = own_length + HIST + jnp.arange(rows, dtype=jnp.int32) // local_rows
    query = (
        rotate_heads(query_normed.reshape(rows, heads_here, HD), positions)
        .astype(jnp.bfloat16)
        .reshape(rows, col_width)
    )
    key_new = (
        rotate_heads(key_normed.reshape(rows, heads_here, HD), positions)
        .astype(jnp.bfloat16)
        .reshape(rows, col_width)
    )
    query_groups = lax.all_gather(query, "req")
    partials = cache_partials(
        query_groups, cache_keys, cache_values, slot_group, slot_index, group_lengths
    )
    arrived = lax.all_to_all(partials, "req", split_axis=0, concat_axis=0, tiled=True)

    keys_all = jnp.concatenate([tail_keys.reshape(local_rows * HIST, col_width), key_new])
    values_all = jnp.concatenate([tail_values.reshape(local_rows * HIST, col_width), value_new])
    spots = jnp.arange(keys_all.shape[0], dtype=jnp.int32)
    sources = ancestry(parents)
    hot = sources[..., None] == spots
    live = jnp.any(hot, axis=2).astype(jnp.float32).reshape(rows, spots.shape[0])
    taking = hot[STEPS - 1].reshape(local_rows * TAIL, spots.shape[0]).astype(jnp.bfloat16)
    out_shape = (local_rows, TAIL, col_width)
    keys_out = (
        jnp.dot(taking, keys_all, preferred_element_type=jnp.float32)
        .astype(jnp.bfloat16)
        .reshape(out_shape)
    )
    values_out = (
        jnp.dot(taking, values_all, preferred_element_type=jnp.float32)
        .astype(jnp.bfloat16)
        .reshape(out_shape)
    )

    context = merge_partials(arrived, query, keys_all, values_all, live)
    attn_part = jnp.dot(context, out_weight, preferred_element_type=jnp.float32)
    hidden = inputs + lax.psum(attn_part, "tp")
    mlp_in = norm_rows(hidden, mlp_gain).astype(jnp.bfloat16)
    mlp_all = lax.all_gather(mlp_in, "req", axis=0, tiled=True)

    logits = jnp.dot(mlp_all, router_weight, preferred_element_type=jnp.float32)
    expert_ids = jnp.arange(experts_all, dtype=jnp.int32)
    named = jnp.any(routes_all[:, :, None] == expert_ids, axis=1)
    chosen = jnp.where(named, logits, floor_value)
    peak = jnp.max(chosen, axis=1, keepdims=True)
    raised = jnp.where(named, jnp.exp(chosen - peak), 0.0)
    probs = raised / jnp.sum(raised, axis=1, keepdims=True)
    activated = []
    for j in range(experts_here):
        share = jnp.sum(
            jnp.where(expert_ids == req_place * experts_here + j, probs, 0.0),
            axis=1,
            keepdims=True,
        )
        gate_and_up = jnp.dot(
            mlp_all,
            gate_up[j].reshape(width, 2 * hidden_here),
            preferred_element_type=jnp.float32,
        )
        product = jax.nn.silu(gate_and_up[:, :hidden_here]) * gate_and_up[:, hidden_here:]
        activated.append((share * product).astype(jnp.bfloat16))
    mixed = jnp.dot(
        jnp.concatenate(activated, axis=1),
        down_weight.reshape(experts_here * hidden_here, width),
        preferred_element_type=jnp.float32,
    ).astype(jnp.bfloat16)
    mixed = lax.psum_scatter(mixed, "req", scatter_dimension=0, tiled=True)
    mixed = lax.psum_scatter(mixed, "tp", scatter_dimension=1, tiled=True)
    own_hidden = lax.dynamic_slice_in_dim(hidden, tp_place * col_width, col_width, 1)
    result = (own_hidden + mixed.astype(jnp.float32)).astype(jnp.bfloat16)
    return (result.reshape(STEPS, local_rows, col_width), keys_out, values_out)


def solution(mesh):
    in_specs = (
        P(None, "req", None),
        P(),
        P(None, None, "tp"),
        P("tp"),
        P("tp"),
        P("tp", None),
        P(),
        P(),
        P("req", None, None, "tp"),
        P("req", "tp", None),
        P("req", "tp"),
        P("req", "tp"),
        P("req", None, "tp"),
        P("req", None, "tp"),
        P(None, "req"),
        P(None, "req", None),
        P(),
        P("req"),
        P("req"),
    )
    out_specs = (P(None, "req", "tp"), P("req", None, "tp"), P("req", None, "tp"))
    return jax.shard_map(body, mesh=mesh, in_specs=in_specs, out_specs=out_specs, check_vma=False)
```

```python
import math

import jax
import jax.numpy as jnp
from jax import lax
from jax.experimental import pallas as pl
from jax.experimental.pallas import tpu as pltpu
from jax.sharding import PartitionSpec as P

HD = 128
BEAMS = 8
PIECE = 128
STEPS = 4
HIST = 4
TAIL = 8
SLOT_BLOCK = 4

eps = 1e-05
floor_value = -1e30
scale = 1.0 / math.sqrt(HD)


def norm_rows(values, scale_gain):
    mean_square = jnp.mean(values * values, axis=-1, keepdims=True)
    return values * lax.rsqrt(mean_square + eps) * scale_gain


def rotate_heads(values, positions):
    half_size = values.shape[-1] // 2
    freqs = jnp.exp(
        jnp.arange(half_size, dtype=jnp.float32) * (-2.0 * math.log(10000.0) / values.shape[-1])
    )
    angles = positions.astype(jnp.float32)[:, None] * freqs[None, :]
    cosine = jnp.cos(angles)[:, None, :]
    sine = jnp.sin(angles)[:, None, :]
    first_half = values[..., :half_size]
    second_half = values[..., half_size:]
    return jnp.concatenate(
        [first_half * cosine - second_half * sine, second_half * cosine + first_half * sine],
        axis=-1,
    )


def dot_t(left, right):
    return lax.dot_general(
        left, right, (((1,), (1,)), ((), ())), preferred_element_type=jnp.float32
    )


def cache_kernel(groups_ref, index_ref, lengths_ref, q_ref, k_ref, v_ref, out_ref, acc):
    rows, cols = q_ref.shape[1], q_ref.shape[2]
    heads = cols // HD
    step = pl.program_id(0)
    lane = lax.broadcasted_iota(jnp.int32, (rows, PIECE), 1)

    @pl.when(step == 0)
    def _():
        @pl.loop(0, q_ref.shape[0])
        def _(g):
            acc[g, :, :cols] = jnp.zeros((rows, cols), jnp.float32)
            acc[g, :, cols:] = jnp.where(lane < heads, floor_value, 0.0)

    found = []
    for j in range(SLOT_BLOCK):
        slot = step * SLOT_BLOCK + j
        group = groups_ref[slot]
        safe = jnp.maximum(group, 0)
        limit = jnp.where(group >= 0, lengths_ref[safe] - index_ref[slot] * PIECE, 0)
        live = lane < limit
        here = pl.ds(j * PIECE, PIECE)
        parts = []
        for h in range(heads):
            cut = pl.ds(h * HD, HD)
            scores = dot_t(q_ref[safe, :, cut], k_ref[here, cut]) * scale
            scores = jnp.where(live, scores, floor_value)
            peak = jnp.max(scores, axis=1, keepdims=True)
            weights = jnp.where(live, jnp.exp(scores - peak), 0.0)
            total = jnp.sum(weights, axis=1, keepdims=True)
            blend = jnp.dot(
                weights.astype(jnp.bfloat16), v_ref[here, cut], preferred_element_type=jnp.float32
            )
            parts.append((peak, total, blend))
        found.append((safe, parts))
    for safe, parts in found:
        stat = acc[safe, :, cols:]
        fresh = stat
        for h, (peak, total, blend) in enumerate(parts):
            cut = pl.ds(h * HD, HD)
            old = stat[:, h : h + 1]
            best = jnp.maximum(old, peak)
            old_factor = jnp.exp(old - best)
            new_factor = jnp.exp(peak - best)
            acc[safe, :, cut] = old_factor * acc[safe, :, cut] + new_factor * blend
            sums = old_factor * stat[:, heads + h : heads + h + 1] + new_factor * total
            fresh = jnp.where(lane == h, best, jnp.where(lane == heads + h, sums, fresh))
        acc[safe, :, cols:] = fresh

    @pl.when(step == pl.num_programs(0) - 1)
    def _():
        words = 2 * heads

        @pl.loop(0, q_ref.shape[0])
        def _(g):
            out_ref[g, :, :cols] = acc[g, :, :cols].astype(jnp.bfloat16)
            stat = acc[g, :, cols:]
            first = stat.astype(jnp.bfloat16).astype(jnp.float32)
            second = (stat - first).astype(jnp.bfloat16).astype(jnp.float32)
            third = stat - first - second
            packed = jnp.where(
                lane < words,
                first,
                jnp.where(
                    lane < 2 * words,
                    pltpu.roll(second, words, 1),
                    jnp.where(lane < 3 * words, pltpu.roll(third, 2 * words, 1), 0.0),
                ),
            )
            out_ref[g, :, cols:] = packed.astype(jnp.bfloat16)


def cache_partials(query_groups, cache_keys, cache_values, slot_group, slot_index, lengths):
    groups, rows, cols = query_groups.shape
    slots = slot_group.shape[0]
    block = SLOT_BLOCK * PIECE
    return pl.pallas_call(
        cache_kernel,
        out_shape=jax.ShapeDtypeStruct((groups, rows, cols + 128), jnp.bfloat16),
        grid_spec=pltpu.PrefetchScalarGridSpec(
            num_scalar_prefetch=3,
            grid=(slots // SLOT_BLOCK,),
            in_specs=[
                pl.BlockSpec((groups, rows, cols), lambda i, *_: (0, 0, 0)),
                pl.BlockSpec((block, cols), lambda i, *_: (i, 0)),
                pl.BlockSpec((block, cols), lambda i, *_: (i, 0)),
            ],
            out_specs=pl.BlockSpec((groups, rows, cols + 128), lambda i, *_: (0, 0, 0)),
            scratch_shapes=[pltpu.VMEM((groups, rows, cols + 128), jnp.float32)],
        ),
    )(slot_group, slot_index, lengths, query_groups, cache_keys, cache_values)


def merge_kernel(part_ref, q_ref, k_ref, v_ref, live_ref, out_ref):
    sources, rows = part_ref.shape[0], part_ref.shape[1]
    cols = q_ref.shape[1]
    heads = cols // HD
    words = 2 * heads
    live = live_ref[...] > 0.5
    stats = []
    for s in range(sources):
        packed = part_ref[s, :, cols:].astype(jnp.float32)
        stats.append(
            packed + pltpu.roll(packed, 128 - words, 1) + pltpu.roll(packed, 128 - 2 * words, 1)
        )
    top = stats[0]
    for s in range(1, sources):
        top = jnp.maximum(top, stats[s])
    for h in range(heads):
        cut = pl.ds(h * HD, HD)
        scores = jnp.where(live, dot_t(q_ref[:, cut], k_ref[:, cut]) * scale, floor_value)
        peak = jnp.max(scores, axis=1, keepdims=True)
        weights = jnp.where(live, jnp.exp(scores - peak), 0.0)
        total = jnp.sum(weights, axis=1, keepdims=True)
        blend = jnp.dot(
            weights.astype(jnp.bfloat16), v_ref[:, cut], preferred_element_type=jnp.float32
        )
        best = jnp.maximum(peak, top[:, h : h + 1])
        factor = jnp.exp(peak - best)
        numer = factor * blend
        denom = factor * total
        for s in range(sources):
            factor = jnp.exp(stats[s][:, h : h + 1] - best)
            numer = numer + factor * part_ref[s, :, cut].astype(jnp.float32)
            denom = denom + factor * stats[s][:, heads + h : heads + h + 1]
        out_ref[:, cut] = (numer / denom).astype(jnp.bfloat16)


def merge_partials(parts, query, keys_all, values_all, live):
    return pl.pallas_call(
        merge_kernel,
        out_shape=jax.ShapeDtypeStruct(query.shape, jnp.bfloat16),
        in_specs=[pl.BlockSpec(memory_space=pltpu.VMEM)] * 5,
        out_specs=pl.BlockSpec(memory_space=pltpu.VMEM),
    )(parts, query, keys_all, values_all, live)


def exchange(values, axis):
    return lax.all_to_all(values, axis, split_axis=0, concat_axis=0, tiled=True)


def send_to_all(values, axis):
    return exchange(jnp.broadcast_to(values, (lax.axis_size(axis),) + values.shape), axis)


def sum_to_owner(values, axis):
    return jnp.sum(exchange(values, axis).astype(jnp.float32), axis=0)


def mix_kernel(act_ref, down_ref, out_ref):
    out_ref[0] = jnp.dot(
        act_ref[...], down_ref[...], preferred_element_type=jnp.float32
    ).astype(jnp.bfloat16)


def mix_columns(activated, down_flat, parts):
    rows, inner = activated.shape
    cols = down_flat.shape[1] // parts
    return pl.pallas_call(
        mix_kernel,
        out_shape=jax.ShapeDtypeStruct((parts, rows, cols), jnp.bfloat16),
        grid=(parts,),
        in_specs=[
            pl.BlockSpec((rows, inner), lambda i: (0, 0)),
            pl.BlockSpec((inner, cols), lambda i: (0, i)),
        ],
        out_specs=pl.BlockSpec((1, rows, cols), lambda i: (i, 0, 0)),
    )(activated, down_flat)


def ancestry(parents):
    beams = jnp.arange(BEAMS, dtype=jnp.int32)

    def follow(table, where):
        return jnp.sum(jnp.where(where[:, None] == beams[None, :], table[None, :], 0), axis=1)

    back = []
    for t in range(STEPS):
        rows = [beams, parents[t]]
        for k in range(2, t + 2):
            rows.append(follow(back[t - 1][k - 1], parents[t]))
        back.append(rows)
    sources = []
    for t in range(STEPS):
        first = back[t][t + 1] * HIST
        columns = [first + j for j in range(HIST)]
        for u in range(STEPS):
            if u <= t:
                columns.append(BEAMS * HIST + u * BEAMS + back[t][t - u])
            else:
                columns.append(jnp.full((BEAMS,), -1, jnp.int32))
        sources.append(jnp.stack(columns, axis=1))
    return jnp.stack(sources)


def body(
    embeds,
    attn_gain,
    qkv_weight,
    query_gain,
    key_gain,
    out_weight,
    mlp_gain,
    router_weight,
    gate_up,
    down_weight,
    cache_keys,
    cache_values,
    tail_keys,
    tail_values,
    parents,
    routes,
    group_lengths,
    slot_group,
    slot_index,
):
    req_place = lax.axis_index("req")
    tp_place = lax.axis_index("tp")
    local_rows = embeds.shape[1]
    width = embeds.shape[2]
    col_width = qkv_weight.shape[2]
    heads_here = col_width // HD
    experts_here = gate_up.shape[0]
    experts_all = router_weight.shape[1]
    hidden_here = gate_up.shape[3]
    rows = STEPS * local_rows

    inputs = embeds.reshape(rows, width).astype(jnp.float32)
    normed = norm_rows(inputs, attn_gain).astype(jnp.bfloat16)
    proj = jnp.dot(
        normed, qkv_weight.reshape(width, 3 * col_width), preferred_element_type=jnp.float32
    )
    query_raw = proj[:, :col_width]
    key_raw = proj[:, col_width : 2 * col_width]
    value_new = proj[:, 2 * col_width :].astype(jnp.bfloat16)
    squares = lax.psum(
        jnp.stack([jnp.sum(query_raw * query_raw, axis=1), jnp.sum(key_raw * key_raw, axis=1)]),
        "tp",
    )
    query_normed = query_raw * lax.rsqrt(squares[0][:, None] / width + eps) * query_gain
    key_normed = key_raw * lax.rsqrt(squares[1][:, None] / width + eps) * key_gain
    own_length = lax.dynamic_index_in_dim(group_lengths, req_place, 0, False)
    positions = own_length + HIST + jnp.arange(rows, dtype=jnp.int32) // local_rows
    query = (
        rotate_heads(query_normed.reshape(rows, heads_here, HD), positions)
        .astype(jnp.bfloat16)
        .reshape(rows, col_width)
    )
    key_new = (
        rotate_heads(key_normed.reshape(rows, heads_here, HD), positions)
        .astype(jnp.bfloat16)
        .reshape(rows, col_width)
    )
    query_groups = send_to_all(query, "req")
    partials = cache_partials(
        query_groups, cache_keys, cache_values, slot_group, slot_index, group_lengths
    )
    arrived = exchange(partials, "req")

    keys_all = jnp.concatenate([tail_keys.reshape(local_rows * HIST, col_width), key_new])
    values_all = jnp.concatenate([tail_values.reshape(local_rows * HIST, col_width), value_new])
    spots = jnp.arange(keys_all.shape[0], dtype=jnp.int32)
    sources = ancestry(parents)
    hot = sources[..., None] == spots
    live = jnp.any(hot, axis=2).astype(jnp.float32).reshape(rows, spots.shape[0])
    taking = hot[STEPS - 1].reshape(local_rows * TAIL, spots.shape[0]).astype(jnp.bfloat16)
    out_shape = (local_rows, TAIL, col_width)
    keys_out = (
        jnp.dot(taking, keys_all, preferred_element_type=jnp.float32)
        .astype(jnp.bfloat16)
        .reshape(out_shape)
    )
    values_out = (
        jnp.dot(taking, values_all, preferred_element_type=jnp.float32)
        .astype(jnp.bfloat16)
        .reshape(out_shape)
    )

    context = merge_partials(arrived, query, keys_all, values_all, live)
    attn_part = jnp.dot(context, out_weight, preferred_element_type=jnp.float32)
    tp_count = lax.axis_size("tp")
    req_count = lax.axis_size("req")
    attn_own = sum_to_owner(attn_part.reshape(tp_count, rows // tp_count, width), "tp")
    hidden = inputs + send_to_all(attn_own, "tp").reshape(rows, width)
    mlp_in = norm_rows(hidden, mlp_gain).astype(jnp.bfloat16)
    mlp_all = lax.all_gather(mlp_in, "req", axis=0, tiled=True)

    logits = jnp.dot(mlp_in, router_weight, preferred_element_type=jnp.float32)
    expert_ids = jnp.arange(experts_all, dtype=jnp.int32)
    named = jnp.any(routes.reshape(rows, -1)[:, :, None] == expert_ids, axis=1)
    chosen = jnp.where(named, logits, floor_value)
    peak = jnp.max(chosen, axis=1, keepdims=True)
    raised = jnp.where(named, jnp.exp(chosen - peak), 0.0)
    probs = raised / jnp.sum(raised, axis=1, keepdims=True)
    shares = exchange(probs.T.reshape(req_count, experts_here, rows), "req")
    activated = []
    for j in range(experts_here):
        share = shares[:, j].reshape(req_count * rows, 1)
        gate_and_up = jnp.dot(
            mlp_all,
            gate_up[j].reshape(width, 2 * hidden_here),
            preferred_element_type=jnp.float32,
        )
        product = jax.nn.silu(gate_and_up[:, :hidden_here]) * gate_and_up[:, hidden_here:]
        activated.append((share * product).astype(jnp.bfloat16))
    mixed = mix_columns(
        jnp.concatenate(activated, axis=1),
        down_weight.reshape(experts_here * hidden_here, width),
        tp_count,
    )
    mixed = sum_to_owner(mixed, "tp").astype(jnp.bfloat16)
    mixed = sum_to_owner(mixed.reshape(req_count, rows, col_width), "req")
    own_hidden = lax.dynamic_slice_in_dim(hidden, tp_place * col_width, col_width, 1)
    result = (own_hidden + mixed).astype(jnp.bfloat16)
    return (result.reshape(STEPS, local_rows, col_width), keys_out, values_out)


def solution(mesh):
    in_specs = (
        P(None, "req", None),
        P(),
        P(None, None, "tp"),
        P("tp"),
        P("tp"),
        P("tp", None),
        P(),
        P(),
        P("req", None, None, "tp"),
        P("req", "tp", None),
        P("req", "tp"),
        P("req", "tp"),
        P("req", None, "tp"),
        P("req", None, "tp"),
        P(None, "req"),
        P(None, "req", None),
        P(),
        P("req"),
        P("req"),
    )
    out_specs = (P(None, "req", "tp"), P("req", None, "tp"), P("req", None, "tp"))
    return jax.shard_map(body, mesh=mesh, in_specs=in_specs, out_specs=out_specs, check_vma=False)
```

```python
import math

import jax
import jax.numpy as jnp
from jax import lax
from jax.experimental import pallas as pl
from jax.experimental.pallas import tpu as pltpu
from jax.sharding import PartitionSpec as P

HD = 128
BEAMS = 8
PIECE = 128
STEPS = 4
HIST = 4
TAIL = 8
SLOT_BLOCK = 8
CHUNKS = 2

eps = 1e-05
floor_value = -1e30
scale = 1.0 / math.sqrt(HD)


def norm_rows(values, scale_gain):
    mean_square = jnp.mean(values * values, axis=-1, keepdims=True)
    return values * lax.rsqrt(mean_square + eps) * scale_gain


def rotate_heads(values, positions):
    half_size = values.shape[-1] // 2
    freqs = jnp.exp(
        jnp.arange(half_size, dtype=jnp.float32) * (-2.0 * math.log(10000.0) / values.shape[-1])
    )
    angles = positions.astype(jnp.float32)[:, None] * freqs[None, :]
    cosine = jnp.cos(angles)[:, None, :]
    sine = jnp.sin(angles)[:, None, :]
    first_half = values[..., :half_size]
    second_half = values[..., half_size:]
    return jnp.concatenate(
        [first_half * cosine - second_half * sine, second_half * cosine + first_half * sine],
        axis=-1,
    )


def dot_t(left, right):
    return lax.dot_general(
        left, right, (((1,), (1,)), ((), ())), preferred_element_type=jnp.float32
    )


def cache_kernel(groups_ref, index_ref, lengths_ref, q_ref, k_ref, v_ref, out_ref, acc):
    rows, cols = q_ref.shape[1], q_ref.shape[2]
    heads = cols // HD
    step = pl.program_id(0)
    lane = lax.broadcasted_iota(jnp.int32, (rows, PIECE), 1)

    @pl.when(step == 0)
    def _():
        @pl.loop(0, q_ref.shape[0])
        def _(g):
            acc[g, :, :cols] = jnp.zeros((rows, cols), jnp.float32)
            acc[g, :, cols:] = jnp.where(lane < heads, floor_value, 0.0)

    found = []
    for j in range(SLOT_BLOCK):
        slot = step * SLOT_BLOCK + j
        group = groups_ref[slot]
        safe = jnp.maximum(group, 0)
        limit = jnp.where(group >= 0, lengths_ref[safe] - index_ref[slot] * PIECE, 0)
        live = lane < limit
        here = pl.ds(j * PIECE, PIECE)
        parts = []
        for h in range(heads):
            cut = pl.ds(h * HD, HD)
            scores = dot_t(q_ref[safe, :, cut], k_ref[here, cut]) * scale
            scores = jnp.where(live, scores, floor_value)
            peak = jnp.max(scores, axis=1, keepdims=True)
            weights = jnp.where(live, jnp.exp(scores - peak), 0.0)
            total = jnp.sum(weights, axis=1, keepdims=True)
            blend = jnp.dot(
                weights.astype(jnp.bfloat16), v_ref[here, cut], preferred_element_type=jnp.float32
            )
            parts.append((peak, total, blend))
        found.append((safe, parts))
    for safe, parts in found:
        stat = acc[safe, :, cols:]
        fresh = stat
        for h, (peak, total, blend) in enumerate(parts):
            cut = pl.ds(h * HD, HD)
            old = stat[:, h : h + 1]
            best = jnp.maximum(old, peak)
            old_factor = jnp.exp(old - best)
            new_factor = jnp.exp(peak - best)
            acc[safe, :, cut] = old_factor * acc[safe, :, cut] + new_factor * blend
            sums = old_factor * stat[:, heads + h : heads + h + 1] + new_factor * total
            fresh = jnp.where(lane == h, best, jnp.where(lane == heads + h, sums, fresh))
        acc[safe, :, cols:] = fresh

    @pl.when(step == pl.num_programs(0) - 1)
    def _():
        words = 2 * heads

        @pl.loop(0, q_ref.shape[0])
        def _(g):
            out_ref[g, :, :cols] = acc[g, :, :cols].astype(jnp.bfloat16)
            stat = acc[g, :, cols:]
            first = stat.astype(jnp.bfloat16).astype(jnp.float32)
            second = (stat - first).astype(jnp.bfloat16).astype(jnp.float32)
            third = stat - first - second
            packed = jnp.where(
                lane < words,
                first,
                jnp.where(
                    lane < 2 * words,
                    pltpu.roll(second, words, 1),
                    jnp.where(lane < 3 * words, pltpu.roll(third, 2 * words, 1), 0.0),
                ),
            )
            out_ref[g, :, cols:] = packed.astype(jnp.bfloat16)


def cache_partials(query_groups, cache_keys, cache_values, slot_group, slot_index, lengths):
    groups, rows, cols = query_groups.shape
    slots = slot_group.shape[0]
    block = SLOT_BLOCK * PIECE
    return pl.pallas_call(
        cache_kernel,
        out_shape=jax.ShapeDtypeStruct((groups, rows, cols + 128), jnp.bfloat16),
        grid_spec=pltpu.PrefetchScalarGridSpec(
            num_scalar_prefetch=3,
            grid=(slots // SLOT_BLOCK,),
            in_specs=[
                pl.BlockSpec((groups, rows, cols), lambda i, *_: (0, 0, 0)),
                pl.BlockSpec((block, cols), lambda i, *_: (i, 0)),
                pl.BlockSpec((block, cols), lambda i, *_: (i, 0)),
            ],
            out_specs=pl.BlockSpec((groups, rows, cols + 128), lambda i, *_: (0, 0, 0)),
            scratch_shapes=[pltpu.VMEM((groups, rows, cols + 128), jnp.float32)],
        ),
    )(slot_group, slot_index, lengths, query_groups, cache_keys, cache_values)


def merge_kernel(part_ref, q_ref, k_ref, v_ref, live_ref, out_ref):
    sources, rows = part_ref.shape[0], part_ref.shape[1]
    cols = q_ref.shape[1]
    heads = cols // HD
    words = 2 * heads
    live = live_ref[...] > 0.5
    stats = []
    for s in range(sources):
        packed = part_ref[s, :, cols:].astype(jnp.float32)
        stats.append(
            packed + pltpu.roll(packed, 128 - words, 1) + pltpu.roll(packed, 128 - 2 * words, 1)
        )
    top = stats[0]
    for s in range(1, sources):
        top = jnp.maximum(top, stats[s])
    for h in range(heads):
        cut = pl.ds(h * HD, HD)
        scores = jnp.where(live, dot_t(q_ref[:, cut], k_ref[:, cut]) * scale, floor_value)
        peak = jnp.max(scores, axis=1, keepdims=True)
        weights = jnp.where(live, jnp.exp(scores - peak), 0.0)
        total = jnp.sum(weights, axis=1, keepdims=True)
        blend = jnp.dot(
            weights.astype(jnp.bfloat16), v_ref[:, cut], preferred_element_type=jnp.float32
        )
        best = jnp.maximum(peak, top[:, h : h + 1])
        factor = jnp.exp(peak - best)
        numer = factor * blend
        denom = factor * total
        for s in range(sources):
            factor = jnp.exp(stats[s][:, h : h + 1] - best)
            numer = numer + factor * part_ref[s, :, cut].astype(jnp.float32)
            denom = denom + factor * stats[s][:, heads + h : heads + h + 1]
        out_ref[:, cut] = (numer / denom).astype(jnp.bfloat16)


def merge_partials(parts, query, keys_all, values_all, live):
    return pl.pallas_call(
        merge_kernel,
        out_shape=jax.ShapeDtypeStruct(query.shape, jnp.bfloat16),
        in_specs=[pl.BlockSpec(memory_space=pltpu.VMEM)] * 5,
        out_specs=pl.BlockSpec(memory_space=pltpu.VMEM),
    )(parts, query, keys_all, values_all, live)


def exchange(values, axis):
    return lax.all_to_all(values, axis, split_axis=0, concat_axis=0, tiled=True)


def send_to_all(values, axis):
    return exchange(jnp.broadcast_to(values, (lax.axis_size(axis),) + values.shape), axis)


def sum_to_owner(values, axis):
    return jnp.sum(exchange(values, axis).astype(jnp.float32), axis=0)


def mix_kernel(act_ref, down_ref, out_ref):
    out_ref[0] = jnp.dot(
        act_ref[...], down_ref[...], preferred_element_type=jnp.float32
    ).astype(jnp.bfloat16)


def mix_columns(activated, down_flat, parts):
    rows, inner = activated.shape
    cols = down_flat.shape[1] // parts
    return pl.pallas_call(
        mix_kernel,
        out_shape=jax.ShapeDtypeStruct((parts, rows, cols), jnp.bfloat16),
        grid=(parts,),
        in_specs=[
            pl.BlockSpec((rows, inner), lambda i: (0, 0)),
            pl.BlockSpec((inner, cols), lambda i: (0, i)),
        ],
        out_specs=pl.BlockSpec((1, rows, cols), lambda i: (i, 0, 0)),
    )(activated, down_flat)


def ancestry(parents):
    beams = jnp.arange(BEAMS, dtype=jnp.int32)

    def follow(table, where):
        return jnp.sum(jnp.where(where[:, None] == beams[None, :], table[None, :], 0), axis=1)

    back = []
    for t in range(STEPS):
        rows = [beams, parents[t]]
        for k in range(2, t + 2):
            rows.append(follow(back[t - 1][k - 1], parents[t]))
        back.append(rows)
    sources = []
    for t in range(STEPS):
        first = back[t][t + 1] * HIST
        columns = [first + j for j in range(HIST)]
        for u in range(STEPS):
            if u <= t:
                columns.append(BEAMS * HIST + u * BEAMS + back[t][t - u])
            else:
                columns.append(jnp.full((BEAMS,), -1, jnp.int32))
        sources.append(jnp.stack(columns, axis=1))
    return jnp.stack(sources)


def body(
    embeds,
    attn_gain,
    qkv_weight,
    query_gain,
    key_gain,
    out_weight,
    mlp_gain,
    router_weight,
    gate_up,
    down_weight,
    cache_keys,
    cache_values,
    tail_keys,
    tail_values,
    parents,
    routes,
    group_lengths,
    slot_group,
    slot_index,
):
    req_place = lax.axis_index("req")
    tp_place = lax.axis_index("tp")
    local_rows = embeds.shape[1]
    width = embeds.shape[2]
    col_width = qkv_weight.shape[2]
    heads_here = col_width // HD
    experts_here = gate_up.shape[0]
    experts_all = router_weight.shape[1]
    hidden_here = gate_up.shape[3]
    rows = STEPS * local_rows

    inputs = embeds.reshape(rows, width).astype(jnp.float32)
    normed = norm_rows(inputs, attn_gain).astype(jnp.bfloat16)
    proj = jnp.dot(
        normed, qkv_weight.reshape(width, 3 * col_width), preferred_element_type=jnp.float32
    )
    query_raw = proj[:, :col_width]
    key_raw = proj[:, col_width : 2 * col_width]
    value_new = proj[:, 2 * col_width :].astype(jnp.bfloat16)
    squares = lax.psum(
        jnp.stack([jnp.sum(query_raw * query_raw, axis=1), jnp.sum(key_raw * key_raw, axis=1)]),
        "tp",
    )
    query_normed = query_raw * lax.rsqrt(squares[0][:, None] / width + eps) * query_gain
    key_normed = key_raw * lax.rsqrt(squares[1][:, None] / width + eps) * key_gain
    own_length = lax.dynamic_index_in_dim(group_lengths, req_place, 0, False)
    positions = own_length + HIST + jnp.arange(rows, dtype=jnp.int32) // local_rows
    query = (
        rotate_heads(query_normed.reshape(rows, heads_here, HD), positions)
        .astype(jnp.bfloat16)
        .reshape(rows, col_width)
    )
    key_new = (
        rotate_heads(key_normed.reshape(rows, heads_here, HD), positions)
        .astype(jnp.bfloat16)
        .reshape(rows, col_width)
    )
    query_groups = send_to_all(query, "req")
    partials = cache_partials(
        query_groups, cache_keys, cache_values, slot_group, slot_index, group_lengths
    )
    arrived = exchange(partials, "req")

    keys_all = jnp.concatenate([tail_keys.reshape(local_rows * HIST, col_width), key_new])
    values_all = jnp.concatenate([tail_values.reshape(local_rows * HIST, col_width), value_new])
    spots = jnp.arange(keys_all.shape[0], dtype=jnp.int32)
    sources = ancestry(parents)
    hot = sources[..., None] == spots
    live = jnp.any(hot, axis=2).astype(jnp.float32).reshape(rows, spots.shape[0])
    taking = hot[STEPS - 1].reshape(local_rows * TAIL, spots.shape[0]).astype(jnp.bfloat16)
    out_shape = (local_rows, TAIL, col_width)
    keys_out = (
        jnp.dot(taking, keys_all, preferred_element_type=jnp.float32)
        .astype(jnp.bfloat16)
        .reshape(out_shape)
    )
    values_out = (
        jnp.dot(taking, values_all, preferred_element_type=jnp.float32)
        .astype(jnp.bfloat16)
        .reshape(out_shape)
    )

    context = merge_partials(arrived, query, keys_all, values_all, live)
    attn_part = jnp.dot(context, out_weight, preferred_element_type=jnp.float32)
    tp_count = lax.axis_size("tp")
    req_count = lax.axis_size("req")
    attn_own = sum_to_owner(attn_part.reshape(tp_count, rows // tp_count, width), "tp")
    hidden = inputs + send_to_all(attn_own, "tp").reshape(rows, width)
    mlp_in = norm_rows(hidden, mlp_gain).astype(jnp.bfloat16)
    chunk = rows // CHUNKS
    gathered = [
        lax.all_gather(mlp_in[c * chunk : (c + 1) * chunk], "req", axis=0, tiled=True)
        for c in range(CHUNKS)
    ]

    logits = jnp.dot(mlp_in, router_weight, preferred_element_type=jnp.float32)
    expert_ids = jnp.arange(experts_all, dtype=jnp.int32)
    named = jnp.any(routes.reshape(rows, -1)[:, :, None] == expert_ids, axis=1)
    chosen = jnp.where(named, logits, floor_value)
    peak = jnp.max(chosen, axis=1, keepdims=True)
    raised = jnp.where(named, jnp.exp(chosen - peak), 0.0)
    probs = raised / jnp.sum(raised, axis=1, keepdims=True)
    shares = exchange(probs.T.reshape(req_count, experts_here, rows), "req")
    down_flat = down_weight.reshape(experts_here * hidden_here, width)
    mixed_chunks = []
    for c in range(CHUNKS):
        activated = []
        for j in range(experts_here):
            share = shares[:, j, c * chunk : (c + 1) * chunk].reshape(req_count * chunk, 1)
            gate_and_up = jnp.dot(
                gathered[c],
                gate_up[j].reshape(width, 2 * hidden_here),
                preferred_element_type=jnp.float32,
            )
            product = jax.nn.silu(gate_and_up[:, :hidden_here]) * gate_and_up[:, hidden_here:]
            activated.append((share * product).astype(jnp.bfloat16))
        mixed = mix_columns(jnp.concatenate(activated, axis=1), down_flat, tp_count)
        mixed = sum_to_owner(mixed, "tp").astype(jnp.bfloat16)
        mixed_chunks.append(mixed.reshape(req_count, chunk, col_width))
    mixed = sum_to_owner(jnp.concatenate(mixed_chunks, axis=1), "req")
    own_hidden = lax.dynamic_slice_in_dim(hidden, tp_place * col_width, col_width, 1)
    result = (own_hidden + mixed).astype(jnp.bfloat16)
    return (result.reshape(STEPS, local_rows, col_width), keys_out, values_out)


def solution(mesh):
    in_specs = (
        P(None, "req", None),
        P(),
        P(None, None, "tp"),
        P("tp"),
        P("tp"),
        P("tp", None),
        P(),
        P(),
        P("req", None, None, "tp"),
        P("req", "tp", None),
        P("req", "tp"),
        P("req", "tp"),
        P("req", None, "tp"),
        P("req", None, "tp"),
        P(None, "req"),
        P(None, "req", None),
        P(),
        P("req"),
        P("req"),
    )
    out_specs = (P(None, "req", "tp"), P("req", None, "tp"), P("req", None, "tp"))
    return jax.shard_map(body, mesh=mesh, in_specs=in_specs, out_specs=out_specs, check_vma=False)
```
